256 devices in a mesh: dp: 16 (over y, z_hi), expert: 8 (over x, core), tensor: 2 (over z_lo).
Axes of the slice: x: 4, y: 4, z: 8 (z_hi: 4, z_lo: 2; z = z_hi * 2 + z_lo), core: 2. Of those that a mesh axis runs over, the one named last changes fastest.
Arguments:
- tokens: bfloat16 [2048, 5120], P('dp', 'tensor'), may hold values from -6 to 6
- routes: int32 [2048, 6], P('dp'), may hold values from 0 to 15, all different within a row; in each aligned block of 128 rows (0 to 127, 128 to 255, ...) at most 72 rows name the same one
- route_weights: float32 [2048, 6], P('dp'), may hold values from 0.05 to 0.5
- gate_weight: bfloat16 [16, 1536, 5120], P('dp', 'expert', 'tensor'), may hold values from -0.078125 to 0.078125
- up_weight: bfloat16 [16, 1536, 5120], P('dp', 'expert', 'tensor'), may hold values from -0.078125 to 0.078125
- down_weight: bfloat16 [16, 1536, 5120], P('dp', 'expert', 'tensor'), may hold values from -0.15625 to 0.15625
- cotangent: bfloat16 [2048, 5120], P('dp', 'tensor'), may hold values from -6 to 6
Outputs:
- layer_out: bfloat16 [2048, 5120], P('dp', 'tensor')
- token_grad: bfloat16 [2048, 5120], P('dp', 'tensor')
- gate_grad: float32 [16, 1536, 5120], P('dp', 'expert', 'tensor')
- up_grad: float32 [16, 1536, 5120], P('dp', 'expert', 'tensor')
- down_grad: float32 [16, 1536, 5120], P('dp', 'expert', 'tensor')
The draws below stay inside these ranges and needn't reach their ends.
Inputs may be any that keep to these rules, and one draw needn't show every extreme that they name: `routes`: each row names 6 different experts. In the rows of one index of dp (aligned blocks of 128 rows) no expert is named by more than 72 rows, a bound that some block reaches.
All inputs are finite; a program needn't handle non-finite values.
Results may differ from the reference program's by a relative error of at most 0.023.
Values may be sent and summed in bfloat16 or wider, within the bound.
A program may use at most 128 MiB of HBM per device.

```python
import math
import jax
import jax.numpy as jnp
import numpy as np
from jax import lax

D = 5120
FF = 1536
TOP = 6
TOK_DP = 128
EXPERTS = 16
TOKENS = 2048
CAP = 72
N_EXPERT = 8


def block_levels(stream_key, extent, pieces, least, largest):
    def one(axis_at, parts):
        draws = jax.random.uniform(jax.random.fold_in(jax.random.fold_in(stream_key, 6), axis_at), (parts,), jnp.float32, least / len(pieces), largest / len(pieces))
        return jnp.repeat(jnp.exp(draws), extent[axis_at] // parts).reshape((-1,) + (1,) * (len(extent) - axis_at - 1))

    level = one(*pieces[0])
    for cut in pieces[1:]:
        level = level * one(*cut)
    return level


def deal_out(key, own, number, rows, amount, top, bound, skew):
    ranking = jax.random.permutation(key, amount)
    crowded, ordinary = portions_of(amount, rows * top, bound, skew, True), portions_of(amount, rows * top, bound, skew, False)
    places = jnp.arange(amount)

    def named(lengths, turn):
        used = int((lengths > 0).sum())
        fixed = max(1, used // 4)
        shifted = fixed + (places - fixed + turn * (used - fixed)) % max(1, amount - fixed)
        return jnp.zeros((amount,), jnp.int32).at[ranking[jnp.where(places < fixed, places, shifted)]].set(jnp.asarray(lengths, jnp.int32))

    lengths = jnp.where(number % 4 == 0, named(crowded, number // 4), named(ordinary, number - number // 4 - 1))
    mixed = jax.random.permutation(jax.random.fold_in(own, 3), amount)
    donor, taker = mixed[0:amount // 2 * 2:2], mixed[1:amount // 2 * 2:2]
    room = jnp.minimum(lengths[donor] - 1, bound - lengths[taker]) // 2
    room = jnp.where((donor == ranking[0]) | (taker == ranking[0]) | (lengths[taker] == 0), 0, jnp.maximum(room, 0))
    shifted = jax.random.randint(jax.random.fold_in(own, 4), (amount // 2,), 0, 1 << 20) % (room + 1)
    lengths = lengths.at[donor].add(-shifted).at[taker].add(shifted)
    items = jnp.searchsorted(jnp.cumsum(lengths), jnp.arange(rows * top), side="right").astype(jnp.int32)
    table = items.reshape(top, rows).T
    table = table[jax.random.permutation(jax.random.fold_in(own, 1), rows)]
    turn = jax.random.randint(jax.random.fold_in(own, 2), (rows, 1), 0, top)
    return jnp.take_along_axis(table, (jnp.arange(top)[None, :] + turn) % top, axis=1)


def portions_of(amount, total, most, skew, full):
    loads = [(1 << 20) // math.isqrt(grade ** skew) + 1 for grade in range(1, amount + 1)]
    largest = most if full else min(most, max(-(-total // amount), total * loads[0] // sum(loads)))
    least = 1 if total - largest >= amount - 1 else 0
    holding, spare = [largest] + [least] * (amount - 1), total - largest - least * (amount - 1)
    while spare > 0:
        free = [i for i in range(1, amount) if holding[i] < largest] or [i for i in range(1, amount) if holding[i] < most]
        mass, left = sum([loads[i] for i in free]), spare
        for i in free:
            extra = min(most - holding[i], max(1, left * loads[i] // mass), spare)
            holding[i] = holding[i] + extra
            spare = spare - extra
    return np.array(holding)


def gaussian(key, extent, spread, limit, shards=(), kind=jnp.bfloat16):
    entries = jax.random.normal(key, extent, jnp.float32) * spread
    if len(shards) > 0:
        entries = block_levels(key, extent, shards, -0.22, 0.18) * entries
    return jnp.clip(entries, min=-limit, max=limit).astype(kind)


def setup_inputs(seed: int = 0) -> dict:
    keys = jax.random.split(jax.random.key(seed), 8)
    tokens = gaussian(keys[0], (TOKENS, D), 1.0, 6.0, ((0, 16), (1, 2)))
    routes_keys = jax.random.split(jax.random.fold_in(keys[1], 1), TOKENS // TOK_DP)
    routes_turns = jax.random.permutation(jax.random.fold_in(keys[1], 3), TOKENS // TOK_DP)
    routes = jax.vmap(lambda own, number: deal_out(jax.random.fold_in(keys[1], 2), own, number, TOK_DP, EXPERTS, TOP, CAP, 2))(routes_keys, routes_turns).reshape((TOKENS, TOP))
    route_weights = jnp.clip(jnp.exp(math.log(0.5) - 2.3025851 * jax.random.uniform(keys[2], (TOKENS, TOP), jnp.float32) ** block_levels(keys[2], (TOKENS, TOP), ((0, 16),), -0.2, 0.2)), 0.05, 0.5)
    gate_weight = gaussian(keys[3], (EXPERTS, FF, D), D ** -0.5, 0.078125, ((0, 16), (1, 8), (2, 2)))
    up_weight = gaussian(keys[4], (EXPERTS, FF, D), D ** -0.5, 0.078125, ((0, 16), (1, 8), (2, 2)))
    down_weight = gaussian(keys[5], (EXPERTS, FF, D), FF ** -0.5, 0.15625, ((0, 16), (1, 8), (2, 2)))
    cotangent = gaussian(keys[6], (TOKENS, D), 1.0, 6.0, ((0, 16), (1, 2)))
    return dict(tokens=tokens, routes=routes, route_weights=route_weights, gate_weight=gate_weight, up_weight=up_weight, down_weight=down_weight, cotangent=cotangent)


def reference(tokens, routes, route_weights, gate_weight, up_weight, down_weight, cotangent):
    share_width = FF // N_EXPERT
    highest = lax.Precision.HIGHEST

    def one_expert(running, expert_id):
        out_acc, grad_acc = running
        matched = routes == expert_id
        pair_coef = jnp.sum(jnp.where(matched, route_weights, jnp.float32(0.0)), axis=1)
        w_gate = gate_weight[expert_id]
        w_upper = up_weight[expert_id]
        w_down = down_weight[expert_id]
        gate_val = jnp.dot(tokens, w_gate.T, preferred_element_type=jnp.float32)
        up_val = jnp.dot(tokens, w_upper.T, preferred_element_type=jnp.float32)
        sigmoid_gate = jax.nn.sigmoid(gate_val)
        activated = gate_val * sigmoid_gate
        hidden = (activated * up_val).astype(jnp.bfloat16)
        partials = jnp.einsum("tsf,sfd->std",
                              hidden.astype(jnp.float32).reshape(TOKENS, N_EXPERT, share_width),
                              w_down.astype(jnp.float32).reshape(N_EXPERT, share_width, D),
                              precision=highest)
        partials = lax.optimization_barrier(partials.astype(jnp.bfloat16))
        expert_out = jnp.sum(partials.astype(jnp.float32), axis=0).astype(jnp.bfloat16)
        out_acc = out_acc + pair_coef[:, None] * expert_out.astype(jnp.float32)
        out_grad = (pair_coef[:, None] * cotangent.astype(jnp.float32)).astype(jnp.bfloat16)
        hidden_grad = jnp.dot(out_grad, w_down.T, preferred_element_type=jnp.float32)
        gate_delta = (hidden_grad * up_val * sigmoid_gate * (1.0 + gate_val * (1.0 - sigmoid_gate))).astype(jnp.bfloat16)
        up_delta = (hidden_grad * activated).astype(jnp.bfloat16)
        row_parts = jnp.einsum("tsf,sfd->std",
                               gate_delta.astype(jnp.float32).reshape(TOKENS, N_EXPERT, share_width),
                               w_gate.astype(jnp.float32).reshape(N_EXPERT, share_width, D),
                               precision=highest)
        row_parts = row_parts + jnp.einsum("tsf,sfd->std",
                                           up_delta.astype(jnp.float32).reshape(TOKENS, N_EXPERT, share_width),
                                           w_upper.astype(jnp.float32).reshape(N_EXPERT, share_width, D),
                                           precision=highest)
        row_parts = lax.optimization_barrier(row_parts.astype(jnp.bfloat16))
        row_grad = jnp.sum(row_parts.astype(jnp.float32), axis=0).astype(jnp.bfloat16)
        grad_acc = grad_acc + row_grad.astype(jnp.float32)
        gate_g = jnp.dot(gate_delta.T, tokens, preferred_element_type=jnp.float32)
        up_g = jnp.dot(up_delta.T, tokens, preferred_element_type=jnp.float32)
        down_g = jnp.dot(hidden.T, out_grad, preferred_element_type=jnp.float32)
        return (out_acc, grad_acc), (gate_g, up_g, down_g)

    start = (jnp.zeros((TOKENS, D), jnp.float32), jnp.zeros((TOKENS, D), jnp.float32))
    (out_acc, grad_acc), (gate_grad, up_grad, down_grad) = lax.scan(
        one_expert, start, jnp.arange(EXPERTS, dtype=jnp.int32))
    return (out_acc.astype(jnp.bfloat16), grad_acc.astype(jnp.bfloat16), gate_grad, up_grad, down_grad)
```

```python
import jax
import jax.numpy as jnp
from jax import lax
from jax.sharding import PartitionSpec as P


def body(tokens, routes, route_weights, gate_weight, up_weight, down_weight, cotangent):
    dp_count = lax.axis_size("dp")
    hidden_split = lax.axis_size("expert")
    gate_weight, up_weight, down_weight = gate_weight[0], up_weight[0], down_weight[0]
    hidden_share, half_width = gate_weight.shape
    tok_rows, top_count = routes.shape
    experts = dp_count
    capacity = min(tok_rows, 3 * tok_rows * top_count // (2 * experts))
    share_rows = capacity // hidden_split
    own_rows = experts * share_rows
    pair_count = tok_rows * top_count

    flat_route = routes.T.reshape(pair_count)
    onehot = (flat_route[:, None] == jnp.arange(experts, dtype=jnp.int32)[None, :])
    running = jnp.cumsum(onehot.astype(jnp.int32), axis=0) - 1
    position = jnp.sum(jnp.where(onehot, running, 0), axis=1)
    target = flat_route * capacity + position
    member = lax.axis_index("expert")
    own_index = jnp.arange(own_rows, dtype=jnp.int32)
    own_slot = (own_index // share_rows) * capacity + member * share_rows + own_index % share_rows
    selector = (own_slot[:, None] == target[None, :]).reshape(own_rows, top_count, tok_rows)
    weight_grid = jnp.sum(
        jnp.where(selector, route_weights.T[None], jnp.float32(0.0)), axis=1
    )
    own_weight = jnp.sum(weight_grid, axis=1, keepdims=True)
    own_place = jnp.any(selector, axis=1).astype(jnp.bfloat16)

    def select(values):
        return jnp.dot(own_place, values, preferred_element_type=jnp.float32)

    def dispatch(rows):
        arrived = lax.all_to_all(
            rows.reshape(dp_count, share_rows, half_width), "dp", split_axis=0, concat_axis=0, tiled=True
        )
        return lax.all_gather(
            arrived.reshape(own_rows, half_width), "expert", axis=0, tiled=True
        )

    def width_sum(partial_values):
        mine = partial_values.astype(jnp.bfloat16)
        other = lax.ppermute(mine, "tensor", [(0, 1), (1, 0)])
        return mine.astype(jnp.float32) + other.astype(jnp.float32)

    def home(partial_rows):
        summed = lax.psum_scatter(
            partial_rows.astype(jnp.bfloat16), "expert", scatter_dimension=0, tiled=True
        )
        returned = lax.all_to_all(
            summed.reshape(dp_count, share_rows, half_width), "dp", split_axis=0, concat_axis=0, tiled=True
        )
        return returned.reshape(own_rows, half_width)

    def token_sum(partial_tokens):
        part = lax.psum_scatter(
            partial_tokens.astype(jnp.bfloat16), "expert", scatter_dimension=0, tiled=True
        )
        return lax.all_gather(part, "expert", axis=0, tiled=True)

    rows = dispatch(select(tokens).astype(jnp.bfloat16))
    grad_rows = dispatch((select(cotangent) * own_weight).astype(jnp.bfloat16))

    nt = (((1,), (1,)), ((), ()))
    nn = (((1,), (0,)), ((), ()))
    tn = (((0,), (0,)), ((), ()))

    def mm(a, b, dims):
        return lax.dot_general(a, b, dims, preferred_element_type=jnp.float32)

    gate_val = width_sum(mm(rows, gate_weight, nt))
    up_val = width_sum(mm(rows, up_weight, nt))
    sigmoid_gate = jax.nn.sigmoid(gate_val)
    activated = gate_val * sigmoid_gate
    hidden = (activated * up_val).astype(jnp.bfloat16)
    expert_out = home(mm(hidden, down_weight, nn))
    out_part = mm(weight_grid.astype(jnp.bfloat16), expert_out, tn)
    layer_out = token_sum(out_part)

    hidden_grad = width_sum(mm(grad_rows, down_weight, nt))
    gate_delta = (
        hidden_grad * up_val * sigmoid_gate * (1.0 + gate_val * (1.0 - sigmoid_gate))
    ).astype(jnp.bfloat16)
    up_delta = (hidden_grad * activated).astype(jnp.bfloat16)
    input_part = mm(gate_delta, gate_weight, nn) + mm(up_delta, up_weight, nn)
    row_grad = home(input_part)
    token_grad = token_sum(mm(own_place, row_grad, tn))
    gate_grad = mm(gate_delta, rows, tn)
    up_grad = mm(up_delta, rows, tn)
    down_grad = mm(hidden, grad_rows, tn)
    return (layer_out, token_grad, gate_grad[None], up_grad[None], down_grad[None])


def solution(mesh):
    in_specs = (
        P("dp", "tensor"),
        P("dp", None),
        P("dp", None),
        P("dp", "expert", "tensor"),
        P("dp", "expert", "tensor"),
        P("dp", "expert", "tensor"),
        P("dp", "tensor"),
    )
    out_specs = (
        P("dp", "tensor"),
        P("dp", "tensor"),
        P("dp", "expert", "tensor"),
        P("dp", "expert", "tensor"),
        P("dp", "expert", "tensor"),
    )
    return jax.shard_map(body, mesh=mesh, in_specs=in_specs, out_specs=out_specs, check_vma=False)
```

```python
import functools

import jax
import jax.numpy as jnp
from jax import lax
from jax.experimental import pallas as pl
from jax.experimental.pallas import tpu as pltpu
from jax.sharding import PartitionSpec as P

MESH = pl.DeviceIdType.MESH
SIDE = 4


def partner(owner, member, j, sign):
    y, z = owner // SIDE, owner % SIDE
    dy = member % 2 + 2 * j
    dz = (member // 2 - dy + SIDE) % SIDE
    if sign < 0:
        dy, dz = SIDE - dy, SIDE - dz
    return (y + dy) % SIDE * SIDE + (z + dz) % SIDE


class Place:
    def __init__(self):
        self.d = lax.axis_index("dp")
        self.h = lax.axis_index("expert")
        self.x, self.c = self.h // 2, self.h % 2
        self.right = self.column((self.x + 1) % SIDE)
        self.left = self.column((self.x + SIDE - 1) % SIDE)
        self.sibling = {"expert": self.x * 2 + 1 - self.c}

    def column(self, x):
        return {"expert": x * 2 + self.c}

    def to(self, j):
        return {"dp": partner(self.d, self.h, j, 1)}

    def back(self, j):
        return {"dp": partner(self.d, self.h, j, -1)}


def remote(src, dst, send, recv, device):
    return pltpu.make_async_remote_copy(
        src_ref=src, dst_ref=dst, send_sem=send, recv_sem=recv, device_id=device, device_id_type=MESH
    )


def greet(devices):
    barrier = pltpu.get_barrier_semaphore()
    for device in devices:
        pl.semaphore_signal(barrier, inc=1, device_id=device, device_id_type=MESH)
    pl.semaphore_wait(barrier, len(devices))


def greet_routes(place, devices, forward):
    barrier = pltpu.get_barrier_semaphore()
    inward = place.back if forward else place.to
    for device in devices + [inward(1)]:
        pl.semaphore_signal(barrier, inc=1, device_id=device, device_id_type=MESH)

    @pl.when(place.h > 0)
    def _():
        pl.semaphore_signal(barrier, inc=1, device_id=inward(0), device_id_type=MESH)

    pl.semaphore_wait(barrier, len(devices) + 1 + jnp.minimum(place.h, 1))


def direct(place, j, src, dst, send, recv, device, act):
    if j == 1:
        copy = remote(src, dst, send, recv, device)
        copy.start() if act == "start" else copy.wait_send()
        return

    @pl.when(place.h > 0)
    def _():
        copy = remote(src, dst, send, recv, device)
        copy.start() if act == "start" else copy.wait_send()

    if act == "start":

        @pl.when(place.h == 0)
        def _():
            pltpu.make_async_copy(src, dst, recv).start()


def landed(ref, sem):
    pltpu.make_async_copy(ref, ref, sem).wait()


def dispatch_kernel(tok, cot, tok_rows, cot_rows, far_send, far_recv, ring_send, ring_recv, sib_send, sib_recv):
    place = Place()
    x, c = place.x, place.c
    greet_routes(place, [place.left, place.right, place.sibling], True)
    inputs, outputs = (tok, cot), (tok_rows, cot_rows)
    home = 2 * place.h
    for a in range(2):
        for j in range(2):
            direct(place, j, inputs[a].at[j], outputs[a].at[home + j], far_send.at[a, j], far_recv.at[a, j], place.to(j), "start")

    pending = []

    def ring(a, block, side, slot):
        ref = outputs[a].at[block]
        copy = remote(ref, ref, ring_send.at[a, side, slot], ring_recv.at[a, side, slot], place.right if side == 0 else place.left)
        copy.start()
        pending.append(copy)

    def share(a, block, slot):
        ref = outputs[a].at[block]
        copy = remote(ref, ref, sib_send.at[a, slot], sib_recv.at[a, slot], place.sibling)
        copy.start()
        pending.append(copy)

    def block_of(shift, j):
        return 2 * ((x + SIDE + shift) % SIDE * 2 + c) + j

    def own(a):
        for j in range(2):
            landed(outputs[a].at[home + j], far_recv.at[a, j])
            ring(a, home + j, 0, j)
            ring(a, home + j, 1, j)
            share(a, home + j, j)

    def near(a):
        for j in range(2):
            for side, shift in ((0, -1), (1, 1)):
                block = block_of(shift, j)
                landed(outputs[a].at[block], ring_recv.at[a, side, j])
                if side == j:
                    ring(a, block, side, 2)
                share(a, block, 2 + 2 * side + j)

    def far(a):
        for side in range(2):
            block = block_of(2, side)
            landed(outputs[a].at[block], ring_recv.at[a, side, 2])
            share(a, block, 6 + side)

    own(0)
    near(0)
    own(1)
    far(0)
    near(1)
    far(1)
    for a in range(2):
        for slot in range(8):
            landed(outputs[a].at[slot], sib_recv.at[a, slot])
        for j in range(2):
            direct(place, j, inputs[a].at[j], outputs[a].at[home + j], far_send.at[a, j], far_recv.at[a, j], place.to(j), "sent")
    for copy in pending:
        copy.wait_send()


def dispatch(tok, cot, rows, width):
    any_spec = pl.BlockSpec(memory_space=pl.ANY)
    full = jax.ShapeDtypeStruct((16, rows, width), jnp.bfloat16)
    dma = pltpu.SemaphoreType.DMA
    return pl.pallas_call(
        dispatch_kernel,
        out_shape=(full, full),
        in_specs=[any_spec] * 2,
        out_specs=(any_spec, any_spec),
        scratch_shapes=[dma((2, 2)), dma((2, 2)), dma((2, 2, 3)), dma((2, 2, 3)), dma((2, 8)), dma((2, 8))],
        compiler_params=pltpu.CompilerParams(collective_id=0, has_side_effects=True),
        name="dispatch",
    )(tok, cot)


def add_blocks(dst, refs, chunk=512):
    width = dst.shape[-1]

    def step(i, carry):
        cols = pl.ds(pl.multiple_of(i * chunk, chunk), chunk)
        total = refs[0][:, cols].astype(jnp.float32)
        for ref in refs[1:]:
            total = total + ref[:, cols].astype(jnp.float32)
        dst[:, cols] = total.astype(dst.dtype)
        return carry

    lax.fori_loop(0, width // chunk, step, 0)


def home_kernel(
    part0, part1, out0, out1, sib0, sib1, sum0, sum1, ring0, ring1, fin0, fin1,
    sib_send, sib_recv, ring_send, ring_recv, far_send, far_recv,
):
    place = Place()
    x, c = place.x, place.c
    greet_routes(place, [place.left, place.right, place.sibling], False)
    parts, outs, sibs, sums, rings, fins = (
        (part0, part1), (out0, out1), (sib0, sib1), (sum0, sum1), (ring0, ring1), (fin0, fin1)
    )
    pending = []
    order = (2, 1, 3, 0)

    def column(shift):
        return (x + shift) % SIDE

    for a in range(2):
        for shift in order:
            for j in range(2):
                slot = 2 * shift + j
                src = parts[a].at[2 * (column(shift) * 2 + 1 - c) + j]
                copy = remote(src, sibs[a].at[slot], sib_send.at[a, slot], sib_recv.at[a, slot], place.sibling)
                copy.start()
                pending.append(copy)

    def send(a, shift, j, side, slot):
        copy = remote(
            sums[a].at[2 * shift + j], rings[a].at[3 * side + slot], ring_send.at[a, side, slot],
            ring_recv.at[a, side, slot], place.right if side == 0 else place.left,
        )
        copy.start()
        pending.append(copy)

    def first(a):
        for shift in order:
            for j in range(2):
                slot = 2 * shift + j
                landed(sibs[a].at[slot], sib_recv.at[a, slot])
                add_blocks(sums[a].at[slot], [parts[a].at[2 * (column(shift) * 2 + c) + j], sibs[a].at[slot]])
                if shift == 2:
                    send(a, 2, j, j, 0)
                elif shift == 1 and j == 1:
                    send(a, 1, 1, 0, 2)
                elif shift == 3 and j == 0:
                    send(a, 3, 0, 1, 1)

    def second(a):
        for side, shift, j, slot in ((0, 1, 0, 1), (1, 3, 1, 2)):
            got = rings[a].at[3 * side]
            landed(got, ring_recv.at[a, side, 0])
            mine = sums[a].at[2 * shift + j]
            add_blocks(mine, [mine, got])
            send(a, shift, j, side, slot)

    def third(a):
        for j in range(2):
            for side in range(2):
                landed(rings[a].at[3 * side + 1 + j], ring_recv.at[a, side, 1 + j])
            add_blocks(fins[a].at[j], [sums[a].at[j], rings[a].at[1 + j], rings[a].at[4 + j]])
            direct(place, j, fins[a].at[j], outs[a].at[j], far_send.at[a, j], far_recv.at[a, j], place.back(j), "start")

    first(0)
    second(0)
    first(1)
    third(0)
    second(1)
    third(1)
    for a in range(2):
        for j in range(2):
            landed(outs[a].at[j], far_recv.at[a, j])
            direct(place, j, fins[a].at[j], outs[a].at[j], far_send.at[a, j], far_recv.at[a, j], place.back(j), "sent")
    for copy in pending:
        copy.wait_send()


def bring_home(part0, part1):
    _, rows, width = part0.shape
    vmem = pl.BlockSpec(memory_space=pltpu.VMEM)

    def blocks(n):
        return jax.ShapeDtypeStruct((n, rows, width), jnp.bfloat16)

    shapes = [blocks(n) for n in (2, 2, 8, 8, 8, 8, 6, 6, 2, 2)]
    dma = pltpu.SemaphoreType.DMA
    return pl.pallas_call(
        home_kernel,
        out_shape=shapes,
        in_specs=[vmem] * 2,
        out_specs=[vmem] * len(shapes),
        scratch_shapes=[dma((2, 8)), dma((2, 8)), dma((2, 2, 3)), dma((2, 2, 3)), dma((2, 2)), dma((2, 2))],
        compiler_params=pltpu.CompilerParams(
            collective_id=1, has_side_effects=True, vmem_limit_bytes=56 * 1024 * 1024
        ),
        name="bring_home",
    )(part0, part1)[:2]


def tail_kernel(part, out, sib, half, got, sib_send, sib_recv, ring_send, ring_recv, all_send, all_recv, back_send, back_recv):
    place = Place()
    x, c = place.x, place.c
    rows = part.shape[1] // 8

    def column(shift):
        return (x + shift) % SIDE

    greet([place.column(column(k)) for k in (1, 2, 3)] + [place.sibling])
    pending = []

    def go(src, dst, send, recv, device):
        copy = remote(src, dst, send, recv, device)
        copy.start()
        pending.append(copy)

    def stripe(col, core):
        return pl.ds(pl.multiple_of((core * SIDE + col) * rows, rows), rows)

    for k in (2, 1, 3, 0):
        go(part.at[:, stripe(column(k), 1 - c)], sib.at[k], sib_send.at[k], sib_recv.at[k], place.sibling)
    for k in (2, 1, 3, 0):
        landed(sib.at[k], sib_recv.at[k])
        for a in range(2):
            add_blocks(half.at[k, a], [part.at[a, stripe(column(k), c)], sib.at[k, a]])
        if k:
            go(half.at[k], got.at[k - 1], ring_send.at[k - 1], ring_recv.at[k - 1], place.column(column(k)))
    for k in range(3):
        landed(got.at[k], ring_recv.at[k])
    mine = out.at[:, stripe(x, c)]
    for a in range(2):
        add_blocks(out.at[a, stripe(x, c)], [half.at[0, a]] + [got.at[k, a] for k in range(3)])
    for k in (2, 1, 3):
        go(mine, mine, all_send.at[k - 1], all_recv.at[k - 1], place.column(column(k)))
    go(mine, mine, back_send.at[0], back_recv.at[0], place.sibling)
    for k in (1, 3, 2):
        ref = out.at[:, stripe(column(SIDE - k), c)]
        landed(ref, all_recv.at[k - 1])
        go(ref, ref, back_send.at[k], back_recv.at[k], place.sibling)
    for k in range(4):
        landed(mine, back_recv.at[k])
    for copy in pending:
        copy.wait_send()


def tail_sum(part):
    _, tokens, width = part.shape
    vmem = pl.BlockSpec(memory_space=pltpu.VMEM)
    rows = tokens // 8

    def shape(*dims):
        return jax.ShapeDtypeStruct(dims, jnp.bfloat16)

    shapes = [shape(2, tokens, width), shape(4, 2, rows, width), shape(4, 2, rows, width), shape(3, 2, rows, width)]
    dma = pltpu.SemaphoreType.DMA
    return pl.pallas_call(
        tail_kernel,
        out_shape=shapes,
        in_specs=[vmem],
        out_specs=[vmem] * len(shapes),
        scratch_shapes=[dma((4,)), dma((4,)), dma((3,)), dma((3,)), dma((3,)), dma((3,)), dma((4,)), dma((4,))],
        compiler_params=pltpu.CompilerParams(collective_id=2, has_side_effects=True),
        name="tail_sum",
    )(part)[0]


def body(tokens, routes, route_weights, gate_weight, up_weight, down_weight, cotangent):
    experts = lax.axis_size("dp")
    gate_weight, up_weight, down_weight = gate_weight[0], up_weight[0], down_weight[0]
    hidden_share, half_width = gate_weight.shape
    tok_rows, top_count = routes.shape
    capacity = min(tok_rows, 3 * tok_rows * top_count // (2 * experts))
    own_rows = 2 * capacity
    pair_count = tok_rows * top_count

    flat_route = routes.T.reshape(pair_count)
    onehot = (flat_route[:, None] == jnp.arange(experts, dtype=jnp.int32)[None, :])
    running = jnp.cumsum(onehot.astype(jnp.int32), axis=0) - 1
    position = jnp.sum(jnp.where(onehot, running, 0), axis=1)
    target = flat_route * capacity + position
    owner, member = lax.axis_index("dp"), lax.axis_index("expert")
    own_index = jnp.arange(own_rows, dtype=jnp.int32)
    own_expert = jnp.where(
        own_index < capacity, partner(owner, member, 0, 1), partner(owner, member, 1, 1)
    )
    own_slot = own_expert * capacity + own_index % capacity
    selector = (own_slot[:, None] == target[None, :]).reshape(own_rows, top_count, tok_rows)
    weight_grid = jnp.sum(
        jnp.where(selector, route_weights.T[None], jnp.float32(0.0)), axis=1
    )
    own_weight = jnp.sum(weight_grid, axis=1, keepdims=True)
    own_place = jnp.any(selector, axis=1).astype(jnp.bfloat16)

    def select(values):
        return jnp.dot(own_place, values, preferred_element_type=jnp.float32)

    def blocks(values):
        return values.astype(jnp.bfloat16).reshape(-1, capacity, half_width)

    def width_sum(partial_values):
        mine = partial_values.astype(jnp.bfloat16)
        other = lax.ppermute(mine, "tensor", [(0, 1), (1, 0)])
        return mine.astype(jnp.float32) + other.astype(jnp.float32)

    rows, grad_rows = dispatch(
        blocks(select(tokens)), blocks(select(cotangent) * own_weight), capacity, half_width
    )
    rows = rows.reshape(experts * capacity, half_width)
    grad_rows = grad_rows.reshape(experts * capacity, half_width)

    nt = (((1,), (1,)), ((), ()))
    nn = (((1,), (0,)), ((), ()))
    tn = (((0,), (0,)), ((), ()))

    def mm(a, b, dims):
        return lax.dot_general(a, b, dims, preferred_element_type=jnp.float32)

    gate_val = width_sum(mm(rows, gate_weight, nt))
    up_val = width_sum(mm(rows, up_weight, nt))
    hidden_grad = width_sum(mm(grad_rows, down_weight, nt))
    sigmoid_gate = jax.nn.sigmoid(gate_val)
    activated = gate_val * sigmoid_gate
    hidden = (activated * up_val).astype(jnp.bfloat16)
    gate_delta = (
        hidden_grad * up_val * sigmoid_gate * (1.0 + gate_val * (1.0 - sigmoid_gate))
    ).astype(jnp.bfloat16)
    up_delta = (hidden_grad * activated).astype(jnp.bfloat16)
    down_part = mm(hidden, down_weight, nn)
    input_part = mm(gate_delta, gate_weight, nn) + mm(up_delta, up_weight, nn)
    expert_out, row_grad = bring_home(blocks(down_part), blocks(input_part))
    out_part = mm(weight_grid.astype(jnp.bfloat16), expert_out.reshape(own_rows, half_width), tn)
    grad_part = mm(own_place, row_grad.reshape(own_rows, half_width), tn)
    both = tail_sum(jnp.stack((out_part, grad_part)).astype(jnp.bfloat16))
    gate_grad = mm(gate_delta, rows, tn)
    up_grad = mm(up_delta, rows, tn)
    down_grad = mm(hidden, grad_rows, tn)
    return (both[0], both[1], gate_grad[None], up_grad[None], down_grad[None])


def solution(mesh):
    in_specs = (
        P("dp", "tensor"),
        P("dp", None),
        P("dp", None),
        P("dp", "expert", "tensor"),
        P("dp", "expert", "tensor"),
        P("dp", "expert", "tensor"),
        P("dp", "tensor"),
    )
    out_specs = (
        P("dp", "tensor"),
        P("dp", "tensor"),
        P("dp", "expert", "tensor"),
        P("dp", "expert", "tensor"),
        P("dp", "expert", "tensor"),
    )
    return jax.shard_map(body, mesh=mesh, in_specs=in_specs, out_specs=out_specs, check_vma=False)
```

```python
import functools

import jax
import jax.numpy as jnp
from jax import lax
from jax.experimental import pallas as pl
from jax.experimental.pallas import tpu as pltpu
from jax.sharding import PartitionSpec as P

MESH = pl.DeviceIdType.MESH
SIDE = 4


def partner(owner, member, j, sign):
    y, z = owner // SIDE, owner % SIDE
    dy = member % 2 + 2 * j
    dz = (member // 2 - dy + SIDE) % SIDE
    if sign < 0:
        dy, dz = SIDE - dy, SIDE - dz
    return (y + dy) % SIDE * SIDE + (z + dz) % SIDE


class Place:
    def __init__(self):
        self.d = lax.axis_index("dp")
        self.h = lax.axis_index("expert")
        self.x, self.c = self.h // 2, self.h % 2
        self.right = self.column((self.x + 1) % SIDE)
        self.left = self.column((self.x + SIDE - 1) % SIDE)
        self.sibling = {"expert": self.x * 2 + 1 - self.c}

    def column(self, x):
        return {"expert": x * 2 + self.c}

    def to(self, j):
        return {"dp": partner(self.d, self.h, j, 1)}

    def back(self, j):
        return {"dp": partner(self.d, self.h, j, -1)}


def remote(src, dst, send, recv, device):
    return pltpu.make_async_remote_copy(
        src_ref=src, dst_ref=dst, send_sem=send, recv_sem=recv, device_id=device, device_id_type=MESH
    )


def greet(devices):
    barrier = pltpu.get_barrier_semaphore()
    for device in devices:
        pl.semaphore_signal(barrier, inc=1, device_id=device, device_id_type=MESH)
    pl.semaphore_wait(barrier, len(devices))


def greet_routes(place, devices, forward):
    barrier = pltpu.get_barrier_semaphore()
    inward = place.back if forward else place.to
    for device in devices + [inward(1)]:
        pl.semaphore_signal(barrier, inc=1, device_id=device, device_id_type=MESH)

    @pl.when(place.h > 0)
    def _():
        pl.semaphore_signal(barrier, inc=1, device_id=inward(0), device_id_type=MESH)

    pl.semaphore_wait(barrier, len(devices) + 1 + jnp.minimum(place.h, 1))


def direct(place, j, src, dst, send, recv, device, act):
    if j == 1:
        copy = remote(src, dst, send, recv, device)
        copy.start() if act == "start" else copy.wait_send()
        return

    @pl.when(place.h > 0)
    def _():
        copy = remote(src, dst, send, recv, device)
        copy.start() if act == "start" else copy.wait_send()

    if act == "start":

        @pl.when(place.h == 0)
        def _():
            pltpu.make_async_copy(src, dst, recv).start()


def landed(ref, sem):
    pltpu.make_async_copy(ref, ref, sem).wait()


def dispatch_kernel(tok, cot, tok_rows, cot_rows, far_send, far_recv, ring_send, ring_recv, sib_send, sib_recv):
    place = Place()
    x, c = place.x, place.c
    greet_routes(place, [place.left, place.right, place.sibling], True)
    inputs, outputs = (tok, cot), (tok_rows, cot_rows)
    home = 2 * place.h
    for a in range(2):
        for j in range(2):
            direct(place, j, inputs[a].at[j], outputs[a].at[home + j], far_send.at[a, j], far_recv.at[a, j], place.to(j), "start")

    pending = []

    def ring(a, block, side, slot):
        ref = outputs[a].at[block]
        copy = remote(ref, ref, ring_send.at[a, side, slot], ring_recv.at[a, side, slot], place.right if side == 0 else place.left)
        copy.start()
        pending.append(copy)

    def share(a, block, slot):
        ref = outputs[a].at[block]
        copy = remote(ref, ref, sib_send.at[a, slot], sib_recv.at[a, slot], place.sibling)
        copy.start()
        pending.append(copy)

    def block_of(shift, j):
        return 2 * ((x + SIDE + shift) % SIDE * 2 + c) + j

    def own(a):
        for j in range(2):
            landed(outputs[a].at[home + j], far_recv.at[a, j])
            ring(a, home + j, 0, j)
            ring(a, home + j, 1, j)
            share(a, home + j, j)

    def near(a):
        for j in range(2):
            for side, shift in ((0, -1), (1, 1)):
                block = block_of(shift, j)
                landed(outputs[a].at[block], ring_recv.at[a, side, j])
                if side == j:
                    ring(a, block, side, 2)
                share(a, block, 2 + 2 * side + j)

    def far(a):
        for side in range(2):
            block = block_of(2, side)
            landed(outputs[a].at[block], ring_recv.at[a, side, 2])
            share(a, block, 6 + side)

    own(0)
    near(0)
    own(1)
    far(0)
    near(1)
    far(1)
    for a in range(2):
        for slot in range(8):
            landed(outputs[a].at[slot], sib_recv.at[a, slot])
        for j in range(2):
            direct(place, j, inputs[a].at[j], outputs[a].at[home + j], far_send.at[a, j], far_recv.at[a, j], place.to(j), "sent")
    for copy in pending:
        copy.wait_send()


def dispatch(tok, cot, rows, width):
    any_spec = pl.BlockSpec(memory_space=pl.ANY)
    full = jax.ShapeDtypeStruct((16, rows, width), jnp.bfloat16)
    dma = pltpu.SemaphoreType.DMA
    return pl.pallas_call(
        dispatch_kernel,
        out_shape=(full, full),
        in_specs=[any_spec] * 2,
        out_specs=(any_spec, any_spec),
        scratch_shapes=[dma((2, 2)), dma((2, 2)), dma((2, 2, 3)), dma((2, 2, 3)), dma((2, 8)), dma((2, 8))],
        compiler_params=pltpu.CompilerParams(collective_id=0, has_side_effects=True),
        name="dispatch",
    )(tok, cot)


def add_blocks(dst, refs, chunk=512):
    width = dst.shape[-1]

    def step(i, carry):
        cols = pl.ds(pl.multiple_of(i * chunk, chunk), chunk)
        total = refs[0][:, cols].astype(jnp.float32)
        for ref in refs[1:]:
            total = total + ref[:, cols].astype(jnp.float32)
        dst[:, cols] = total.astype(dst.dtype)
        return carry

    lax.fori_loop(0, width // chunk, step, 0)


def home_kernel(
    part0, part1, left0, left1, left2, rows, grad_rows,
    out0, out1, sib0, sib1, sum0, sum1, ring0, ring1, fin0, fin1, grad0, grad1, grad2,
    sib_send, sib_recv, ring_send, ring_recv, far_send, far_recv, right_rows, weight_sum, load_sem, store_sem,
):
    place = Place()
    x, c = place.x, place.c
    lefts, grads = (left0, left1, left2), (grad0, grad1, grad2)
    loads = [pltpu.make_async_copy(src, right_rows, load_sem) for src in (rows, grad_rows)]
    stores = [pltpu.make_async_copy(weight_sum.at[i], grads[i], store_sem.at[i]) for i in range(3)]
    loads[0].start()

    def weight_grad(i, chunk=512):
        if i != 1:
            loads[i // 2].wait()

        def step(k, carry):
            cols = pl.ds(pl.multiple_of(k * chunk, chunk), chunk)
            weight_sum[i, :, cols] = jnp.dot(
                lefts[i][...], right_rows[:, cols], preferred_element_type=jnp.float32
            )
            return carry

        lax.fori_loop(0, right_rows.shape[1] // chunk, step, 0)
        stores[i].start()
        if i == 1:
            loads[1].start()

    greet_routes(place, [place.left, place.right, place.sibling], False)
    parts, outs, sibs, sums, rings, fins = (
        (part0, part1), (out0, out1), (sib0, sib1), (sum0, sum1), (ring0, ring1), (fin0, fin1)
    )
    pending = []
    order = (2, 1, 3, 0)

    def column(shift):
        return (x + shift) % SIDE

    for a in range(2):
        for shift in order:
            for j in range(2):
                slot = 2 * shift + j
                src = parts[a].at[2 * (column(shift) * 2 + 1 - c) + j]
                copy = remote(src, sibs[a].at[slot], sib_send.at[a, slot], sib_recv.at[a, slot], place.sibling)
                copy.start()
                pending.append(copy)

    def send(a, shift, j, side, slot):
        copy = remote(
            sums[a].at[2 * shift + j], rings[a].at[3 * side + slot], ring_send.at[a, side, slot],
            ring_recv.at[a, side, slot], place.right if side == 0 else place.left,
        )
        copy.start()
        pending.append(copy)

    def first(a):
        for shift in order:
            for j in range(2):
                slot = 2 * shift + j
                landed(sibs[a].at[slot], sib_recv.at[a, slot])
                add_blocks(sums[a].at[slot], [parts[a].at[2 * (column(shift) * 2 + c) + j], sibs[a].at[slot]])
                if shift == 2:
                    send(a, 2, j, j, 0)
                elif shift == 1 and j == 1:
                    send(a, 1, 1, 0, 2)
                elif shift == 3 and j == 0:
                    send(a, 3, 0, 1, 1)

    def second(a):
        for side, shift, j, slot in ((0, 1, 0, 1), (1, 3, 1, 2)):
            got = rings[a].at[3 * side]
            landed(got, ring_recv.at[a, side, 0])
            mine = sums[a].at[2 * shift + j]
            add_blocks(mine, [mine, got])
            send(a, shift, j, side, slot)

    def third(a):
        for j in range(2):
            for side in range(2):
                landed(rings[a].at[3 * side + 1 + j], ring_recv.at[a, side, 1 + j])
            add_blocks(fins[a].at[j], [sums[a].at[j], rings[a].at[1 + j], rings[a].at[4 + j]])
            direct(place, j, fins[a].at[j], outs[a].at[j], far_send.at[a, j], far_recv.at[a, j], place.back(j), "start")

    first(0)
    weight_grad(0)
    second(0)
    first(1)
    weight_grad(1)
    third(0)
    second(1)
    weight_grad(2)
    third(1)
    for a in range(2):
        for j in range(2):
            landed(outs[a].at[j], far_recv.at[a, j])
            direct(place, j, fins[a].at[j], outs[a].at[j], far_send.at[a, j], far_recv.at[a, j], place.back(j), "sent")
    for copy in pending:
        copy.wait_send()
    for copy in stores:
        copy.wait()


def bring_home(part0, part1, lefts, token_rows, grad_rows):
    _, rows, width = part0.shape
    share, slots = lefts[0].shape
    any_spec = pl.BlockSpec(memory_space=pl.ANY)
    vmem = pl.BlockSpec(memory_space=pltpu.VMEM)

    def blocks(n):
        return jax.ShapeDtypeStruct((n, rows, width), jnp.bfloat16)

    shapes = [blocks(n) for n in (2, 2, 8, 8, 8, 8, 6, 6, 2, 2)]
    dma = pltpu.SemaphoreType.DMA
    grad_shapes = [jax.ShapeDtypeStruct((share, width), jnp.float32)] * 3
    results = pl.pallas_call(
        home_kernel,
        out_shape=shapes + grad_shapes,
        in_specs=[vmem] * 5 + [any_spec] * 2,
        out_specs=[vmem] * len(shapes) + [any_spec] * 3,
        scratch_shapes=[
            dma((2, 8)), dma((2, 8)), dma((2, 2, 3)), dma((2, 2, 3)), dma((2, 2)), dma((2, 2)),
            pltpu.VMEM((slots, width), jnp.bfloat16), pltpu.VMEM((3, share, width), jnp.float32), dma, dma((3,)),
        ],
        compiler_params=pltpu.CompilerParams(
            collective_id=1, has_side_effects=True, vmem_limit_bytes=58 * 1024 * 1024
        ),
        name="bring_home",
    )(part0, part1, *lefts, token_rows, grad_rows)
    return results[:2], results[-3:]


def tail_kernel(
    part0, part1, out0, out1, sib, half, got,
    sib_send, sib_recv, ring_send, ring_recv, all_send, all_recv, back_send, back_recv,
):
    place = Place()
    x, c = place.x, place.c
    parts, outs = (part0, part1), (out0, out1)
    rows = part0.shape[0] // 8

    def column(shift):
        return (x + shift) % SIDE

    greet([place.column(column(k)) for k in (1, 2, 3)] + [place.sibling])
    pending = []

    def go(src, dst, send, recv, device):
        copy = remote(src, dst, send, recv, device)
        copy.start()
        pending.append(copy)

    def stripe(col, core):
        return pl.ds(pl.multiple_of((core * SIDE + col) * rows, rows), rows)

    for k in (2, 1, 3, 0):
        for a in range(2):
            src = parts[a].at[stripe(column(k), 1 - c)]
            go(src, sib.at[k, a], sib_send.at[a, k], sib_recv.at[a, k], place.sibling)
    for k in (2, 1, 3, 0):
        for a in range(2):
            landed(sib.at[k, a], sib_recv.at[a, k])
            add_blocks(half.at[k, a], [parts[a].at[stripe(column(k), c)], sib.at[k, a]])
        if k:
            go(half.at[k], got.at[k - 1], ring_send.at[k - 1], ring_recv.at[k - 1], place.column(column(k)))
    for k in range(3):
        landed(got.at[k], ring_recv.at[k])
    mine = [out.at[stripe(x, c)] for out in outs]
    for a in range(2):
        add_blocks(mine[a], [half.at[0, a]] + [got.at[k, a] for k in range(3)])
        for k in (2, 1, 3):
            go(mine[a], mine[a], all_send.at[a, k - 1], all_recv.at[a, k - 1], place.column(column(k)))
        go(mine[a], mine[a], back_send.at[a, 0], back_recv.at[a, 0], place.sibling)
    for a in range(2):
        for k in (1, 3, 2):
            ref = outs[a].at[stripe(column(SIDE - k), c)]
            landed(ref, all_recv.at[a, k - 1])
            go(ref, ref, back_send.at[a, k], back_recv.at[a, k], place.sibling)
    for a in range(2):
        for k in range(4):
            landed(mine[a], back_recv.at[a, k])
    for copy in pending:
        copy.wait_send()


def tail_sum(part0, part1):
    tokens, width = part0.shape
    vmem = pl.BlockSpec(memory_space=pltpu.VMEM)
    rows = tokens // 8

    def shape(*dims):
        return jax.ShapeDtypeStruct(dims, jnp.bfloat16)

    shapes = [shape(tokens, width), shape(tokens, width), shape(4, 2, rows, width), shape(4, 2, rows, width), shape(3, 2, rows, width)]
    dma = pltpu.SemaphoreType.DMA
    return pl.pallas_call(
        tail_kernel,
        out_shape=shapes,
        in_specs=[vmem] * 2,
        out_specs=[vmem] * len(shapes),
        scratch_shapes=[dma((2, 4)), dma((2, 4)), dma((3,)), dma((3,)), dma((2, 3)), dma((2, 3)), dma((2, 4)), dma((2, 4))],
        compiler_params=pltpu.CompilerParams(collective_id=2, has_side_effects=True),
        name="tail_sum",
    )(part0, part1)[:2]


def body(tokens, routes, route_weights, gate_weight, up_weight, down_weight, cotangent):
    experts = lax.axis_size("dp")
    gate_weight, up_weight, down_weight = gate_weight[0], up_weight[0], down_weight[0]
    hidden_share, half_width = gate_weight.shape
    tok_rows, top_count = routes.shape
    capacity = min(tok_rows, 3 * tok_rows * top_count // (2 * experts))
    own_rows = 2 * capacity
    pair_count = tok_rows * top_count

    flat_route = routes.T.reshape(pair_count)
    onehot = (flat_route[:, None] == jnp.arange(experts, dtype=jnp.int32)[None, :])
    running = jnp.cumsum(onehot.astype(jnp.int32), axis=0) - 1
    position = jnp.sum(jnp.where(onehot, running, 0), axis=1)
    target = flat_route * capacity + position
    owner, member = lax.axis_index("dp"), lax.axis_index("expert")
    own_index = jnp.arange(own_rows, dtype=jnp.int32)
    own_expert = jnp.where(
        own_index < capacity, partner(owner, member, 0, 1), partner(owner, member, 1, 1)
    )
    own_slot = own_expert * capacity + own_index % capacity
    selector = (own_slot[:, None] == target[None, :]).reshape(own_rows, top_count, tok_rows)
    weight_grid = jnp.sum(
        jnp.where(selector, route_weights.T[None], jnp.float32(0.0)), axis=1
    )
    own_weight = jnp.sum(weight_grid, axis=1, keepdims=True)
    own_place = jnp.any(selector, axis=1).astype(jnp.bfloat16)

    def select(values):
        return jnp.dot(own_place, values, preferred_element_type=jnp.float32)

    def blocks(values):
        return values.astype(jnp.bfloat16).reshape(-1, capacity, half_width)

    def width_sum(partial_values):
        mine = partial_values.astype(jnp.bfloat16)
        other = lax.ppermute(mine, "tensor", [(0, 1), (1, 0)])
        return mine.astype(jnp.float32) + other.astype(jnp.float32)

    rows, grad_rows = dispatch(
        blocks(select(tokens)), blocks(select(cotangent) * own_weight), capacity, half_width
    )
    rows = rows.reshape(experts * capacity, half_width)
    grad_rows = grad_rows.reshape(experts * capacity, half_width)

    nt = (((1,), (1,)), ((), ()))
    nn = (((1,), (0,)), ((), ()))
    tn = (((0,), (0,)), ((), ()))

    def mm(a, b, dims):
        return lax.dot_general(a, b, dims, preferred_element_type=jnp.float32)

    gate_val = width_sum(mm(rows, gate_weight, nt))
    up_val = width_sum(mm(rows, up_weight, nt))
    hidden_grad = width_sum(mm(grad_rows, down_weight, nt))
    sigmoid_gate = jax.nn.sigmoid(gate_val)
    activated = gate_val * sigmoid_gate
    hidden = (activated * up_val).astype(jnp.bfloat16)
    gate_delta = (
        hidden_grad * up_val * sigmoid_gate * (1.0 + gate_val * (1.0 - sigmoid_gate))
    ).astype(jnp.bfloat16)
    up_delta = (hidden_grad * activated).astype(jnp.bfloat16)
    down_part = mm(hidden, down_weight, nn)
    input_part = mm(gate_delta, gate_weight, nn) + mm(up_delta, up_weight, nn)
    (expert_out, row_grad), (gate_grad, up_grad, down_grad) = bring_home(
        blocks(down_part), blocks(input_part), (gate_delta.T, up_delta.T, hidden.T), rows, grad_rows
    )
    out_part = mm(weight_grid.astype(jnp.bfloat16), expert_out.reshape(own_rows, half_width), tn)
    grad_part = mm(own_place, row_grad.reshape(own_rows, half_width), tn)
    both = tail_sum(out_part.astype(jnp.bfloat16), grad_part.astype(jnp.bfloat16))
    return (both[0], both[1], gate_grad[None], up_grad[None], down_grad[None])


def solution(mesh):
    in_specs = (
        P("dp", "tensor"),
        P("dp", None),
        P("dp", None),
        P("dp", "expert", "tensor"),
        P("dp", "expert", "tensor"),
        P("dp", "expert", "tensor"),
        P("dp", "tensor"),
    )
    out_specs = (
        P("dp", "tensor"),
        P("dp", "tensor"),
        P("dp", "expert", "tensor"),
        P("dp", "expert", "tensor"),
        P("dp", "expert", "tensor"),
    )
    return jax.shard_map(body, mesh=mesh, in_specs=in_specs, out_specs=out_specs, check_vma=False)
```
